32 devices in a mesh: clip: 8 (over y, x, core), tm: 4 (over z).
Axes of the slice: x: 2, y: 2, z: 4, core: 2. Of those that a mesh axis runs over, the one named last changes fastest.
Arguments:
- features: bfloat16 [16, 4, 64, 1024], P('clip', 'tm'), may hold values from -6 to 6
- flow_forward: int32 [16, 4, 2, 16], P('clip', 'tm'), may hold values from -4 to 4
- flow_backward: int32 [16, 4, 2, 16], P('clip', 'tm'), may hold values from -4 to 4
- w_forward_in: bfloat16 [64, 1152], replicated, may hold values from -0.1875 to 0.1875
- b_forward_in: float32 [64], replicated, may hold values from -3 to 3
- w_forward_out: bfloat16 [64, 576], replicated, may hold values from -0.25 to 0.25
- b_forward_out: float32 [64], replicated, may hold values from -3 to 3
- w_backward_in: bfloat16 [64, 1152], replicated, may hold values from -0.1875 to 0.1875
- b_backward_in: float32 [64], replicated, may hold values from -3 to 3
- w_backward_out: bfloat16 [64, 576], replicated, may hold values from -0.25 to 0.25
- b_backward_out: float32 [64], replicated, may hold values from -3 to 3
- w_merge: bfloat16 [64, 1152], replicated, may hold values from -0.1875 to 0.1875
- b_merge: float32 [64], replicated, may hold values from -3 to 3
- w_head: bfloat16 [48, 64], replicated, may hold values from -0.75 to 0.75
- b_head: float32 [48], replicated, may hold values from -3 to 3
- target: bfloat16 [16, 4, 48, 1024], P('clip', 'tm'), may hold values from -24 to 24
Outputs:
- restored: bfloat16 [16, 4, 48, 1024], P('clip', 'tm')
- grad_merge: float32 [64, 1152], replicated
- grad_head: float32 [48, 64], replicated
- loss: float32 [], replicated
The draws below stay inside these ranges and needn't reach their ends.
All inputs are finite; a program needn't handle non-finite values.
Results may differ from the reference program's by a relative error of at most 0.0085.
Values may be sent and summed in bfloat16 or wider, within the bound.
A program may use at most 64 MiB of HBM per device.

```python
import math
import jax
import jax.numpy as jnp
from jax import lax

CHANNELS = 64
SUBPIX = 48
PATCH_ROWS = 32
PATCH_COLS = 32
PIXELS = 1024
BLOCKS = 16
CLIPS = 16
FRAMES = 4


def draw_target(key, part):
    noise_key, level_key, sign_key = jax.random.split(key, 3)
    full_shape = (CLIPS, FRAMES, SUBPIX, PIXELS)
    offset_shape = (CLIPS, FRAMES, SUBPIX, 1)
    noise = jax.random.truncated_normal(noise_key, -6.0, 6.0, full_shape, jnp.float32)
    level = jnp.exp(jax.random.uniform(level_key, offset_shape, jnp.float32, math.log(2.0), math.log(16.0)))
    sign_draw = jax.random.uniform(sign_key, offset_shape, jnp.float32, 0.0, 1.0)
    signed = jnp.where(sign_draw < 0.5, -level, level)
    return (noise + signed).astype(jnp.bfloat16)


def touch_ends(drawn, key, smallest, largest):
    index_at = [jax.random.randint(jax.random.fold_in(key, axis), (), 0, length) for axis, length in enumerate(drawn.shape)]
    main_axis = drawn.shape.index(max(drawn.shape))
    next_to = index_at[:main_axis] + [(index_at[main_axis] + 1) % drawn.shape[main_axis]] + index_at[main_axis + 1:]
    return drawn.at[tuple(index_at)].set(smallest).at[tuple(next_to)].set(largest)


def shard_levels(stream_key, extent, cuts, smallest, high):
    level = 1.0
    for axis_at, parts in cuts:
        steps = jax.random.uniform(jax.random.fold_in(jax.random.fold_in(stream_key, 6), axis_at), (parts,), jnp.float32, smallest / len(cuts), high / len(cuts))
        level = level * jnp.repeat(jnp.exp(steps), extent[axis_at] // parts).reshape((-1,) + (1,) * (len(extent) - 1 - axis_at))
    return level


def normal_values(own_key, dims, spread, bound, cuts=(), held_as=jnp.bfloat16):
    values = spread * jax.random.normal(own_key, dims, jnp.float32)
    if cuts:
        values = values * shard_levels(own_key, dims, cuts, -0.22, 0.18)
    return jnp.clip(values, -bound, bound).astype(held_as)


def setup_inputs(seed: int = 0) -> dict:
    key_list = jax.random.split(jax.random.key(seed), 17)
    return {
        "features": normal_values(key_list[0], (CLIPS, FRAMES, CHANNELS, PIXELS), 1.0, 6.0, ((0, 8), (1, 4))),
        "flow_forward": touch_ends(jax.random.randint(key_list[1], (CLIPS, FRAMES, 2, BLOCKS), -4, 5), jax.random.fold_in(key_list[1], 1), -4, 4).astype(jnp.int32),
        "flow_backward": touch_ends(jax.random.randint(key_list[2], (CLIPS, FRAMES, 2, BLOCKS), -4, 5), jax.random.fold_in(key_list[2], 1), -4, 4).astype(jnp.int32),
        "w_forward_in": normal_values(key_list[3], (CHANNELS, 18 * CHANNELS), (18 * CHANNELS) ** -0.5, 0.1875),
        "b_forward_in": normal_values(key_list[4], (CHANNELS,), 0.5, 3.0, (), jnp.float32),
        "w_forward_out": normal_values(key_list[5], (CHANNELS, 9 * CHANNELS), (9 * CHANNELS) ** -0.5, 0.25),
        "b_forward_out": normal_values(key_list[6], (CHANNELS,), 0.5, 3.0, (), jnp.float32),
        "w_backward_in": normal_values(key_list[7], (CHANNELS, 18 * CHANNELS), (18 * CHANNELS) ** -0.5, 0.1875),
        "b_backward_in": normal_values(key_list[8], (CHANNELS,), 0.5, 3.0, (), jnp.float32),
        "w_backward_out": normal_values(key_list[9], (CHANNELS, 9 * CHANNELS), (9 * CHANNELS) ** -0.5, 0.25),
        "b_backward_out": normal_values(key_list[10], (CHANNELS,), 0.5, 3.0, (), jnp.float32),
        "w_merge": normal_values(key_list[11], (CHANNELS, 18 * CHANNELS), (18 * CHANNELS) ** -0.5, 0.1875),
        "b_merge": normal_values(key_list[12], (CHANNELS,), 0.5, 3.0, (), jnp.float32),
        "w_head": normal_values(key_list[13], (SUBPIX, CHANNELS), CHANNELS ** -0.5, 0.75),
        "b_head": normal_values(key_list[14], (SUBPIX,), 0.5, 3.0, (), jnp.float32),
        "target": draw_target(jax.random.fold_in(key_list[16], 71), 0),
    }


flow_reach = 4
tile_rows = 8
block_side = 8
clip_limit = 128.0
leak_slope = 0.1

def stack_taps(source, height, width):
    channels = source.shape[0]
    picture = source.reshape(channels, height, width)
    padded = jnp.pad(picture, ((0, 0), (1, 1), (1, 1)))
    layers = [padded[:, row_off:row_off + height, col_off:col_off + width] for row_off in range(3) for col_off in range(3)]
    return jnp.concatenate(layers, axis=0).reshape(9 * channels, height * width)

def warp_state(hidden_state, flow_map, height, width):
    channels = hidden_state.shape[0]
    picture = hidden_state.reshape(channels, height, width)
    padded = jnp.pad(picture, ((0, 0), (flow_reach, flow_reach), (0, 0)))
    grid_shape = (height // block_side, width // block_side)
    shift_rows = jnp.repeat(jnp.repeat(flow_map[0].reshape(grid_shape), block_side, 0), block_side, 1)
    shift_cols = jnp.repeat(jnp.repeat(flow_map[1].reshape(grid_shape), block_side, 0), block_side, 1)
    row_pos = lax.broadcasted_iota(jnp.int32, (height, width), 0)
    col_pos = lax.broadcasted_iota(jnp.int32, (height, width), 1)
    source_col = col_pos + shift_cols
    inside = (source_col >= 0) & (source_col < width)
    window_rows = tile_rows + 2 * flow_reach
    pieces = []
    for tile_index in range(height // tile_rows):
        row_start = tile_index * tile_rows
        window = padded[:, row_start:row_start + window_rows, :].reshape(channels, window_rows * width)
        local_row = row_pos[row_start:row_start + tile_rows] + shift_rows[row_start:row_start + tile_rows] - row_start + flow_reach
        target_cell = local_row * width + source_col[row_start:row_start + tile_rows]
        target_cell = jnp.where(inside[row_start:row_start + tile_rows], target_cell, -1).reshape(-1)
        window_cell = lax.broadcasted_iota(jnp.int32, (window_rows * width, tile_rows * width), 0)
        one_hot = (window_cell == target_cell[None, :]).astype(jnp.bfloat16)
        pieces.append(jnp.dot(window, one_hot, preferred_element_type=jnp.float32))
    return jnp.concatenate(pieces, axis=1).astype(jnp.bfloat16)

def propagate(prior_state, feature, flow_map, weights, height, width):
    w_first, b_first, w_second, b_second = weights
    warped = warp_state(prior_state, flow_map, height, width)
    joined = jnp.concatenate([warped, feature], axis=0)
    first_out = jnp.dot(w_first, stack_taps(joined, height, width), preferred_element_type=jnp.float32) + b_first[:, None]
    first_out = jax.nn.leaky_relu(first_out, leak_slope).astype(jnp.bfloat16)
    second_out = jnp.dot(w_second, stack_taps(first_out, height, width), preferred_element_type=jnp.float32) + b_second[:, None]
    return (warped.astype(jnp.float32) + second_out).astype(jnp.bfloat16)

def merge_and_grade(fwd_state, bwd_state, target_frame, merge_weights, height, width, loss_scale):
    w_merge, b_merge, w_head, b_head = merge_weights
    joined = jnp.concatenate([fwd_state, bwd_state], axis=0)
    columns = stack_taps(joined, height, width)
    mixed_pre = jnp.dot(w_merge, columns, preferred_element_type=jnp.float32) + b_merge[:, None]
    sigmoid_part = jax.nn.sigmoid(mixed_pre)
    active = (mixed_pre * sigmoid_part).astype(jnp.bfloat16)
    output = jnp.dot(w_head, active, preferred_element_type=jnp.float32) + b_head[:, None]
    misfit = output - target_frame.astype(jnp.float32)
    loss_part = 0.5 * loss_scale * jnp.sum(misfit * misfit)
    errors = (misfit * loss_scale).astype(jnp.bfloat16)
    grad_head = lax.dot_general(errors, active, (((1,), (1,)), ((), ())), preferred_element_type=jnp.float32)
    back_grad = lax.dot_general(w_head, errors, (((0,), (0,)), ((), ())), preferred_element_type=jnp.float32)
    silu_slope = sigmoid_part * (1.0 + mixed_pre * (1.0 - sigmoid_part))
    d_mixed = (back_grad * silu_slope).astype(jnp.bfloat16)
    grad_merge = lax.dot_general(d_mixed, columns, (((1,), (1,)), ((), ())), preferred_element_type=jnp.float32)
    return (output.astype(jnp.bfloat16), grad_merge, grad_head, loss_part)

def reference(features, flow_forward, flow_backward, w_forward_in, b_forward_in, w_forward_out, b_forward_out, w_backward_in, b_backward_in, w_backward_out, b_backward_out, w_merge, b_merge, w_head, b_head, target):
    fwd_weights = (w_forward_in, b_forward_in, w_forward_out, b_forward_out)
    bwd_weights = (w_backward_in, b_backward_in, w_backward_out, b_backward_out)
    merge_weights = (w_merge, b_merge, w_head, b_head)
    loss_scale = 1.0 / (CLIPS * FRAMES)

    def one_clip(totals, inputs):
        clip_feats, clip_fwd, clip_bwd, clip_target = inputs
        prior_state = jnp.zeros((CHANNELS, PIXELS), jnp.bfloat16)
        forward_list = []
        for frame_index in range(FRAMES):
            prior_state = propagate(prior_state, clip_feats[frame_index], clip_fwd[frame_index], fwd_weights, PATCH_ROWS, PATCH_COLS)
            forward_list.append(prior_state)
        prior_state = jnp.zeros((CHANNELS, PIXELS), jnp.bfloat16)
        backward_list = [prior_state] * FRAMES
        for frame_index in range(FRAMES - 1, -1, -1):
            prior_state = propagate(prior_state, clip_feats[frame_index], clip_bwd[frame_index], bwd_weights, PATCH_ROWS, PATCH_COLS)
            backward_list[frame_index] = prior_state
        outputs = []
        for frame_index in range(FRAMES):
            frame_out, grad_merge, grad_head, loss_part = merge_and_grade(forward_list[frame_index], backward_list[frame_index], clip_target[frame_index], merge_weights, PATCH_ROWS, PATCH_COLS, loss_scale)
            totals = (totals[0] + grad_merge, totals[1] + grad_head, totals[2] + loss_part)
            outputs.append(frame_out)
        return (totals, jnp.stack(outputs))
    initial = (jnp.zeros((CHANNELS, 18 * CHANNELS), jnp.float32), jnp.zeros((SUBPIX, CHANNELS), jnp.float32), jnp.zeros((), jnp.float32))
    totals, restored = lax.scan(one_clip, initial, (features, flow_forward, flow_backward, target))
    squares = jnp.sum(totals[0] * totals[0]) + jnp.sum(totals[1] * totals[1])
    factor = jnp.minimum(1.0, clip_limit / jnp.sqrt(squares + 1e-06))
    return (restored, totals[0] * factor, totals[1] * factor, totals[2])
```

```python
import functools

import jax
import jax.numpy as jnp
from jax import lax
from jax.experimental import pallas as pl
from jax.experimental.pallas import tpu as pltpu
from jax.sharding import PartitionSpec as P

CHANNELS = 64
SUBPIX = 48
WIDTH = 32
PIXELS = 1024
BLOCK = 8
REACH = 4
TILE = 256
MARGIN = REACH * WIDTH
WINDOW = TILE + 2 * MARGIN
CLIP_LIMIT = 128.0
LEAK = 0.1
PACK_ROWS = 256
PACK_COLS = 384
MESH = pl.DeviceIdType.MESH
BF = jnp.bfloat16
F32 = jnp.float32


def roll_lanes(value, shift):
    return pltpu.roll(value, shift % PIXELS, 1)


def lane_masks():
    lane = lax.broadcasted_iota(jnp.int32, (1, PIXELS), 1)
    col = lane % WIDTH
    return (
        (col != 0),
        (col != WIDTH - 1),
        (lane >= WIDTH),
        (lane < PIXELS - WIDTH),
    )


def column_taps(value, masks):
    left = jnp.where(masks[0], roll_lanes(value, 1), 0.0)
    right = jnp.where(masks[1], roll_lanes(value, -1), 0.0)
    return [left.astype(BF), value.astype(BF), right.astype(BF)]


def row_sum(stacked, masks):
    up = jnp.where(masks[2], roll_lanes(stacked[:CHANNELS], WIDTH), 0.0)
    down = jnp.where(masks[3], roll_lanes(stacked[2 * CHANNELS :], -WIDTH), 0.0)
    return up + stacked[CHANNELS : 2 * CHANNELS] + down


def dot(a, b):
    return jnp.dot(a, b, preferred_element_type=F32)


def dot_t(a, b):
    return lax.dot_general(a, b, (((1,), (1,)), ((), ())), preferred_element_type=F32)


def stack_rows(weight):
    third = weight.shape[1] // 3
    return jnp.concatenate([weight[:, i * third : (i + 1) * third] for i in range(3)], axis=0)


def propagate(state, cells, feature, w_in, b_in, w_out, b_out, masks):
    window_cell = lax.broadcasted_iota(jnp.int32, (WINDOW, TILE), 0)
    pieces = []
    for start in range(0, PIXELS, TILE):
        one_hot = (window_cell == cells[:, start : start + TILE]).astype(F32).astype(BF)
        pieces.append(dot(state[:, start : start + WINDOW], one_hot))
    warped = jnp.concatenate(pieces, axis=1)
    taps_g = column_taps(warped, masks)
    taps_x = column_taps(feature.astype(F32), masks)
    joined = jnp.concatenate([t for pair in zip(taps_g, taps_x) for t in pair], axis=0)
    hidden = row_sum(dot(w_in, joined), masks) + b_in
    hidden = jnp.where(hidden >= 0, hidden, LEAK * hidden).astype(BF).astype(F32)
    taps_a = jnp.concatenate(column_taps(hidden, masks), axis=0)
    update = row_sum(dot(w_out, taps_a), masks) + b_out
    return (warped + update).astype(BF)


def merge(hf, hb, target, w_merge, b_merge, w_head, b_head, scale, masks):
    taps_f = column_taps(hf.astype(F32), masks)
    taps_b = column_taps(hb.astype(F32), masks)
    joined = jnp.concatenate([t for pair in zip(taps_f, taps_b) for t in pair], axis=0)
    m = row_sum(dot(w_merge, joined), masks) + b_merge
    sig = jax.nn.sigmoid(m)
    active = (m * sig).astype(BF)
    out = dot(w_head, active) + b_head
    misfit = out - target.astype(F32)
    loss = jnp.sum(misfit * misfit, axis=0, keepdims=True)
    loss = jnp.sum(loss, axis=1, keepdims=True) * (0.5 * scale)
    err = (misfit * scale).astype(BF)
    g_head = dot_t(err, active)
    back = lax.dot_general(w_head, err, (((0,), (0,)), ((), ())), preferred_element_type=F32)
    d_m = (back * (sig * (1.0 + m * (1.0 - sig)))).astype(BF).astype(F32)
    above = jnp.where(masks[3], roll_lanes(d_m, -WIDTH), 0.0).astype(BF)
    below = jnp.where(masks[2], roll_lanes(d_m, WIDTH), 0.0).astype(BF)
    g_merge = dot_t(jnp.concatenate([above, d_m.astype(BF), below], axis=0), joined)
    return out.astype(BF), g_merge, g_head, loss


def gather_kernel(sections, feat_ref, cell_ref, feat_out, cell_out, local_sem, send_sem, recv_sem):
    me = lax.axis_index("tm")
    barrier = pltpu.get_barrier_semaphore()
    for off in range(1, sections):
        pl.semaphore_signal(
            barrier, 1, device_id={"tm": lax.rem(me + off, sections)}, device_id_type=MESH
        )
    pl.semaphore_wait(barrier, sections - 1)
    copies = []
    for k, (src, dst) in enumerate(((cell_ref, cell_out), (feat_ref, feat_out))):
        for off in range(1, sections):
            copies.append(
                pltpu.make_async_remote_copy(
                    src,
                    dst.at[me],
                    send_sem.at[k, off],
                    recv_sem.at[k, off],
                    device_id={"tm": lax.rem(me + off, sections)},
                    device_id_type=MESH,
                )
            )
        copies.append(pltpu.make_async_copy(src, dst.at[me], local_sem.at[k]))
    for copy in copies:
        copy.start()
    for copy in copies:
        copy.wait()


def compute_kernel(
    sections,
    scale,
    feat_ref,
    cell_ref,
    wfi,
    bfi,
    wfo,
    bfo,
    wbi,
    bbi,
    wbo,
    bbo,
    wm,
    bm,
    wh,
    bh,
    target,
    out_ref,
    pack_ref,
    state,
    w_in,
    b_in,
    w_out,
    b_out,
):
    clips = target.shape[0]
    me = lax.axis_index("tm")
    masks = lane_masks()
    state[...] = jnp.zeros_like(state)
    for d, (wi, bi, wo, bo) in enumerate(((wfi, bfi, wfo, bfo), (wbi, bbi, wbo, bbo))):
        w_in[d] = stack_rows(wi[...])
        w_out[d] = stack_rows(wo[...])
        b_in[d] = bi[...]
        b_out[d] = bo[...]

    def turn(i, carry):
        forward = i <= me
        d = jnp.where(forward, 0, 1)
        frame = jnp.where(forward, i, sections + me - i)
        made = [
            propagate(
                state.at[d, c],
                cell_ref[frame, pl.ds(d * clips + c, 1), :],
                feat_ref[frame, c],
                w_in[d],
                b_in[d],
                w_out[d],
                b_out[d],
                masks,
            )
            for c in range(clips)
        ]
        for c in range(clips):
            state[d, c, :, MARGIN : MARGIN + PIXELS] = made[c]
        return carry

    lax.fori_loop(0, sections + 1, turn, 0)
    w_merge = stack_rows(wm[...])
    total = None
    for c in range(clips):
        inner = slice(MARGIN, MARGIN + PIXELS)
        out, *grads = merge(
            state[0, c, :, inner],
            state[1, c, :, inner],
            target[c],
            w_merge,
            bm[...],
            wh[...],
            bh[...],
            scale,
            masks,
        )
        out_ref[c] = out
        total = grads if total is None else [a + b for a, b in zip(total, grads)]
    rows = 3 * CHANNELS
    pack_ref[rows:, :] = jnp.zeros((PACK_ROWS - rows, PACK_COLS), F32)
    pack_ref[:rows, :] = total[0]
    pack_ref[rows : rows + SUBPIX, :CHANNELS] = total[1]
    pack_ref[rows + SUBPIX :, 128:256] = jnp.broadcast_to(
        total[2], (PACK_ROWS - rows - SUBPIX, 128)
    )


def reduce_kernel(
    group,
    sections,
    x_ref,
    gm_ref,
    gh_ref,
    loss_ref,
    got,
    part,
    full,
    send1,
    recv1,
    send2,
    recv2,
    send3,
    recv3,
):
    rows = PACK_ROWS // group
    me = lax.axis_index("clip")
    sec = lax.axis_index("tm")
    barrier = pltpu.get_barrier_semaphore()
    for off in range(1, group):
        pl.semaphore_signal(
            barrier, 1, device_id={"clip": lax.rem(me + off, group)}, device_id_type=MESH
        )
    for off in range(1, sections):
        pl.semaphore_signal(
            barrier, 1, device_id={"tm": lax.rem(sec + off, sections)}, device_id_type=MESH
        )
    pl.semaphore_wait(barrier, group + sections - 2)

    def chunk(i):
        return pl.ds(pl.multiple_of(i * rows, rows), rows)

    copies = []
    for off in range(1, group):
        peer = lax.rem(me + off, group)
        copies.append(
            pltpu.make_async_remote_copy(
                x_ref.at[chunk(peer)],
                got.at[off],
                send1.at[off],
                recv1.at[off],
                device_id={"clip": peer},
                device_id_type=MESH,
            )
        )
    for copy in copies:
        copy.start()
    total = x_ref[chunk(me)]
    for off, copy in enumerate(copies, 1):
        copy.wait()
        total = total + got[off]
    part[sec] = total
    copies = []
    for off in range(1, sections):
        copies.append(
            pltpu.make_async_remote_copy(
                part.at[sec],
                part.at[sec],
                send2.at[off],
                recv2.at[off],
                device_id={"tm": lax.rem(sec + off, sections)},
                device_id_type=MESH,
            )
        )
    for copy in copies:
        copy.start()
    for copy in copies:
        copy.wait()
    total = part[0]
    for s in range(1, sections):
        total = total + part[s]
    full[chunk(me)] = total
    copies = []
    for off in range(1, group):
        copies.append(
            pltpu.make_async_remote_copy(
                full.at[chunk(me)],
                full.at[chunk(me)],
                send3.at[off],
                recv3.at[off],
                device_id={"clip": lax.rem(me + off, group)},
                device_id_type=MESH,
            )
        )
    for copy in copies:
        copy.start()
    for copy in copies:
        copy.wait()
    top = 3 * CHANNELS
    g_merge = full[:top, :]
    g_head = full[top : top + SUBPIX, :CHANNELS]

    def squares(v):
        return jnp.sum(jnp.sum(v * v, axis=0, keepdims=True), axis=1, keepdims=True)

    factor = jnp.minimum(1.0, CLIP_LIMIT / jnp.sqrt(squares(g_merge) + squares(g_head) + 1e-06))
    for i in range(3):
        gm_ref[:, i * PACK_COLS : (i + 1) * PACK_COLS] = (
            g_merge[i * CHANNELS : (i + 1) * CHANNELS] * factor
        )
    gh_ref[...] = g_head * factor
    loss_ref[...] = full[top + SUBPIX : top + SUBPIX + 1, 128:129]


def window_cells(flow):
    side = WIDTH // BLOCK
    grid = flow.reshape(flow.shape[0], 2, PIXELS // (WIDTH * BLOCK), side)
    wide = jnp.repeat(jnp.repeat(grid, BLOCK, 2), BLOCK, 3)
    row = lax.broadcasted_iota(jnp.int32, wide.shape[2:], 0)
    col = lax.broadcasted_iota(jnp.int32, wide.shape[2:], 1)
    source_col = col + wide[:, 1]
    local_row = row % BLOCK + wide[:, 0] + REACH
    cell = jnp.where(
        (source_col >= 0) & (source_col < WIDTH), local_row * WIDTH + source_col, -1
    )
    return cell.reshape(flow.shape[0], PIXELS)


def on_device(
    features,
    flow_forward,
    flow_backward,
    w_forward_in,
    b_forward_in,
    w_forward_out,
    b_forward_out,
    w_backward_in,
    b_backward_in,
    w_backward_out,
    b_backward_out,
    w_merge,
    b_merge,
    w_head,
    b_head,
    target,
):
    clips = features.shape[0]
    sections = lax.axis_size("tm")
    group = lax.axis_size("clip")
    scale = 1.0 / (clips * group * sections)
    flows = jnp.concatenate([flow_forward[:, 0], flow_backward[:, 0]], axis=0)
    cells = window_cells(flows)
    anywhere = pl.BlockSpec(memory_space=pl.ANY)
    vmem = pl.BlockSpec(memory_space=pltpu.VMEM)
    dma = pltpu.SemaphoreType.DMA
    all_feats, all_cells = pl.pallas_call(
        functools.partial(gather_kernel, sections),
        out_shape=(
            jax.ShapeDtypeStruct((sections, clips, CHANNELS, PIXELS), BF),
            jax.ShapeDtypeStruct((sections, 2 * clips, PIXELS), jnp.int32),
        ),
        in_specs=[anywhere] * 2,
        out_specs=[anywhere] * 2,
        scratch_shapes=[dma((2,)), dma((2, sections)), dma((2, sections))],
        compiler_params=pltpu.CompilerParams(collective_id=0, has_side_effects=True),
        name="gather",
    )(features[:, 0], cells)
    column = lambda b: b[:, None]
    restored, pack = pl.pallas_call(
        functools.partial(compute_kernel, sections, scale),
        out_shape=(
            jax.ShapeDtypeStruct((clips, SUBPIX, PIXELS), BF),
            jax.ShapeDtypeStruct((PACK_ROWS, PACK_COLS), F32),
        ),
        in_specs=[vmem] * 15,
        out_specs=[vmem] * 2,
        scratch_shapes=[
            pltpu.VMEM((2, clips, CHANNELS, PIXELS + 2 * MARGIN), BF),
            pltpu.VMEM((2, 3 * CHANNELS, 6 * CHANNELS), BF),
            pltpu.VMEM((2, CHANNELS, 1), F32),
            pltpu.VMEM((2, 3 * CHANNELS, 3 * CHANNELS), BF),
            pltpu.VMEM((2, CHANNELS, 1), F32),
        ],
        compiler_params=pltpu.CompilerParams(vmem_limit_bytes=48 << 20),
        name="compute",
    )(
        all_feats,
        all_cells,
        w_forward_in,
        column(b_forward_in),
        w_forward_out,
        column(b_forward_out),
        w_backward_in,
        column(b_backward_in),
        w_backward_out,
        column(b_backward_out),
        w_merge,
        column(b_merge),
        w_head,
        column(b_head),
        target[:, 0],
    )
    rows = PACK_ROWS // group
    grad_merge, grad_head, loss = pl.pallas_call(
        functools.partial(reduce_kernel, group, sections),
        out_shape=(
            jax.ShapeDtypeStruct((CHANNELS, 18 * CHANNELS), F32),
            jax.ShapeDtypeStruct((SUBPIX, CHANNELS), F32),
            jax.ShapeDtypeStruct((1, 1), F32),
        ),
        in_specs=[vmem],
        out_specs=[vmem] * 3,
        scratch_shapes=[
            pltpu.VMEM((group, rows, PACK_COLS), F32),
            pltpu.VMEM((sections, rows, PACK_COLS), F32),
            pltpu.VMEM((PACK_ROWS, PACK_COLS), F32),
            dma((group,)),
            dma((group,)),
            dma((sections,)),
            dma((sections,)),
            dma((group,)),
            dma((group,)),
        ],
        compiler_params=pltpu.CompilerParams(collective_id=1, has_side_effects=True),
        name="reduce",
    )(pack)
    return (restored[:, None], grad_merge, grad_head, loss[0, 0])


def solution(mesh):
    split = P("clip", "tm", None, None)
    in_specs = (split,) * 3 + (P(),) * 12 + (split,)
    out_specs = (split, P(), P(), P())
    return jax.shard_map(
        on_device, mesh=mesh, in_specs=in_specs, out_specs=out_specs, check_vma=False
    )
```

```python
import functools

import jax
import jax.numpy as jnp
from jax import lax
from jax.experimental import pallas as pl
from jax.experimental.pallas import tpu as pltpu
from jax.sharding import PartitionSpec as P

CHANNELS = 64
SUBPIX = 48
WIDTH = 32
PIXELS = 1024
BLOCK = 8
REACH = 4
TILE = 256
MARGIN = REACH * WIDTH
WINDOW = TILE + 2 * MARGIN
CLIP_LIMIT = 128.0
LEAK = 0.1
PACK_ROWS = 256
PACK_COLS = 384
MESH = pl.DeviceIdType.MESH
BF = jnp.bfloat16
F32 = jnp.float32
PART_TYPE = F32


def roll_lanes(value, shift):
    return pltpu.roll(value, shift % PIXELS, 1)


def lane_masks():
    lane = lax.broadcasted_iota(jnp.int32, (1, PIXELS), 1)
    col = lane % WIDTH
    return (
        (col != 0),
        (col != WIDTH - 1),
        (lane >= WIDTH),
        (lane < PIXELS - WIDTH),
    )


def column_taps(value, masks):
    left = jnp.where(masks[0], roll_lanes(value, 1), 0.0)
    right = jnp.where(masks[1], roll_lanes(value, -1), 0.0)
    return [left.astype(BF), value.astype(BF), right.astype(BF)]


def row_sum(stacked, masks):
    up = jnp.where(masks[2], roll_lanes(stacked[:CHANNELS], WIDTH), 0.0)
    down = jnp.where(masks[3], roll_lanes(stacked[2 * CHANNELS :], -WIDTH), 0.0)
    return up + stacked[CHANNELS : 2 * CHANNELS] + down


def dot(a, b):
    return jnp.dot(a, b, preferred_element_type=F32)


def dot_t(a, b):
    return lax.dot_general(a, b, (((1,), (1,)), ((), ())), preferred_element_type=F32)


def stack_rows(weight):
    third = weight.shape[1] // 3
    return jnp.concatenate([weight[:, i * third : (i + 1) * third] for i in range(3)], axis=0)


def merge(hf, hb, target, w_merge, b_merge, w_head, b_head, scale, masks):
    taps_f = column_taps(hf.astype(F32), masks)
    taps_b = column_taps(hb.astype(F32), masks)
    joined = jnp.concatenate([t for pair in zip(taps_f, taps_b) for t in pair], axis=0)
    m = row_sum(dot(w_merge, joined), masks) + b_merge
    sig = jax.nn.sigmoid(m)
    active = (m * sig).astype(BF)
    out = dot(w_head, active) + b_head
    misfit = out - target.astype(F32)
    loss = jnp.sum(misfit * misfit, axis=0, keepdims=True)
    loss = jnp.sum(loss, axis=1, keepdims=True) * (0.5 * scale)
    err = (misfit * scale).astype(BF)
    g_head = dot_t(err, active)
    back = lax.dot_general(w_head, err, (((0,), (0,)), ((), ())), preferred_element_type=F32)
    d_m = (back * (sig * (1.0 + m * (1.0 - sig)))).astype(BF).astype(F32)
    above = jnp.where(masks[3], roll_lanes(d_m, -WIDTH), 0.0).astype(BF)
    below = jnp.where(masks[2], roll_lanes(d_m, WIDTH), 0.0).astype(BF)
    g_merge = dot_t(jnp.concatenate([above, d_m.astype(BF), below], axis=0), joined)
    return out.astype(BF), g_merge, g_head, loss


def window_cells(flow_ref, clip, start):
    lane = lax.broadcasted_iota(jnp.int32, (1, TILE), 1)
    row, col = lane // WIDTH, lane % WIDTH
    side = WIDTH // BLOCK
    first = start // TILE * side

    def offsets(part):
        value = jnp.full((1, TILE), flow_ref[clip, 0, part, first], jnp.int32)
        for b in range(1, side):
            value = jnp.where(col >= b * BLOCK, flow_ref[clip, 0, part, first + b], value)
        return value

    source_col = col + offsets(1)
    cell = (row + offsets(0) + REACH) * WIDTH + source_col
    return jnp.where((source_col >= 0) & (source_col < WIDTH), cell, -1)


def fused_kernel(group, sections, scale, *refs):
    n_in = 14
    flows = refs[:2]
    hbm_in = refs[2 : 2 + n_in]
    out_ref, gm_ref, gh_ref, loss_ref = refs[2 + n_in : 6 + n_in]
    held = refs[6 + n_in : 6 + 2 * n_in]
    (
        in_sem,
        out_buf,
        out_sem,
        w_g,
        w_x,
        w_out,
        b_in,
        b_out,
        one_hot,
        fixed,
        prior,
        state,
        hop_send,
        hop_recv,
        acc_gm,
        acc_gh,
        acc_loss,
        pack,
        got,
        part,
        full,
        send1,
        recv1,
        send2,
        recv2,
        send3,
        recv3,
    ) = refs[6 + 2 * n_in :]
    feat, wfi, bfi, wfo, bfo, wbi, bbi, wbo, bbo, wm, bm, wh, bh, target = held
    clips = feat.shape[0]
    rows = PACK_ROWS // group
    me = lax.axis_index("clip")
    sec = lax.axis_index("tm")

    loads = [
        pltpu.make_async_copy(a, b, in_sem.at[k]) for k, (a, b) in enumerate(zip(hbm_in, held))
    ]
    for load in loads:
        load.start()
    prior[...] = jnp.zeros_like(prior)
    barrier = pltpu.get_barrier_semaphore()
    for off in range(1, group):
        pl.semaphore_signal(
            barrier, 1, device_id={"clip": lax.rem(me + off, group)}, device_id_type=MESH
        )
    for off in range(1, sections):
        pl.semaphore_signal(
            barrier, 1, device_id={"tm": lax.rem(sec + off, sections)}, device_id_type=MESH
        )
    for load in loads:
        load.wait()

    masks = lane_masks()
    eye = lax.broadcasted_iota(jnp.int32, (CHANNELS, CHANNELS), 0) == lax.broadcasted_iota(
        jnp.int32, (CHANNELS, CHANNELS), 1
    )

    def column(row):
        n = row.shape[1]
        return jnp.sum(jnp.where(eye[:n, :n], row, 0.0), axis=1, keepdims=True)

    def part_rows(weight, first):
        return jnp.concatenate(
            [
                jnp.concatenate(
                    [
                        weight[:, (3 * dy + dx) * 128 + first : (3 * dy + dx) * 128 + first + 64]
                        for dx in range(3)
                    ],
                    axis=1,
                )
                for dy in range(3)
            ],
            axis=0,
        )

    for d, (wi, bi, wo, bo) in enumerate(((wfi, bfi, wfo, bfo), (wbi, bbi, wbo, bbo))):
        w_g[d] = part_rows(wi[...], 0)
        w_x[d] = part_rows(wi[...], CHANNELS)
        w_out[d] = stack_rows(wo[...])
        b_in[d] = column(bi[...])
        b_out[d] = column(bo[...])
    pl.semaphore_wait(barrier, group + sections - 2)

    window_cell = lax.broadcasted_iota(jnp.int32, (WINDOW, TILE), 0)
    inner = pl.ds(MARGIN, PIXELS)

    def hop(d, c):
        slot = d * clips + c
        return pltpu.make_async_remote_copy(
            state.at[d, c],
            prior.at[d, c, :, inner],
            hop_send.at[slot],
            hop_recv.at[slot],
            device_id={"tm": sec + 1 - 2 * d},
            device_id_type=MESH,
        )

    def place(d):
        return jnp.where(d == 0, sec, sections - 1 - sec)

    def step(d, c):
        for k, start in enumerate(range(0, PIXELS, TILE)):
            cells = jnp.where(
                d == 0, window_cells(flows[0], c, start), window_cells(flows[1], c, start)
            )
            one_hot[k] = (window_cell == cells).astype(F32).astype(BF)
        taps_x = jnp.concatenate(column_taps(feat[c, 0].astype(F32), masks), axis=0)
        fixed[...] = row_sum(dot(w_x[d], taps_x), masks) + b_in[d]

        @pl.when(place(d) > 0)
        def _():
            hop(d, c).wait_recv()

        warped = jnp.concatenate(
            [
                dot(prior[d, c, :, start : start + WINDOW], one_hot[start // TILE])
                for start in range(0, PIXELS, TILE)
            ],
            axis=1,
        )
        taps_g = jnp.concatenate(column_taps(warped, masks), axis=0)
        hidden = row_sum(dot(w_g[d], taps_g), masks) + fixed[...]
        hidden = jnp.where(hidden >= 0, hidden, LEAK * hidden).astype(BF).astype(F32)
        taps_a = jnp.concatenate(column_taps(hidden, masks), axis=0)
        update = row_sum(dot(w_out[d], taps_a), masks) + b_out[d]
        state[d, c] = (warped + update).astype(BF)

        @pl.when(place(d) < sections - 1)
        def _():
            hop(d, c).start()

    early = jnp.where(2 * sec < sections, 0, 1)

    def first_turn(c, carry):
        step(early, c)
        return carry

    lax.fori_loop(0, clips, first_turn, 0)
    acc_gm[...] = jnp.zeros_like(acc_gm)
    acc_gh[...] = jnp.zeros_like(acc_gh)
    acc_loss[...] = jnp.zeros_like(acc_loss)
    w_merge = stack_rows(wm[...])
    b_merge = column(bm[...])
    b_head = column(bh[...])

    def store_out(c):
        return pltpu.make_async_copy(out_buf.at[c], out_ref.at[c, 0], out_sem.at[c])

    def last_turn(c, carry):
        step(1 - early, c)
        out, g_merge, g_head, loss = merge(
            state[0, c],
            state[1, c],
            target[c, 0],
            w_merge,
            b_merge,
            wh[...],
            b_head,
            scale,
            masks,
        )
        out_buf[c] = out
        store_out(c).start()
        acc_gm[...] += g_merge
        acc_gh[...] += g_head
        acc_loss[...] += loss
        return carry

    lax.fori_loop(0, clips, last_turn, 0)

    top = 3 * CHANNELS
    g_merge = acc_gm[...]
    extra = jnp.concatenate(
        [
            jnp.concatenate(
                [acc_gh[...], jnp.zeros((SUBPIX, CHANNELS), F32)],
                axis=1,
            ),
            jnp.broadcast_to(acc_loss[...], (PACK_ROWS - top - SUBPIX, 128)),
        ],
        axis=0,
    )
    extra = jnp.concatenate(
        [extra, jnp.zeros((PACK_ROWS - top, PACK_COLS - 128), F32)], axis=1
    )
    packed = jnp.concatenate([g_merge, extra], axis=0)
    for g in range(group):
        pack[g] = packed[g * rows : (g + 1) * rows].astype(pack.dtype)

    copies = []
    for off in range(1, group):
        peer = lax.rem(me + off, group)
        copies.append(
            pltpu.make_async_remote_copy(
                pack.at[peer],
                got.at[off],
                send1.at[off],
                recv1.at[off],
                device_id={"clip": peer},
                device_id_type=MESH,
            )
        )
    for copy in copies:
        copy.start()
    total = pack[me].astype(F32)
    for off, copy in enumerate(copies, 1):
        copy.wait_recv()
        total = total + got[off].astype(F32)
    part[sec] = total.astype(part.dtype)
    more = []
    for off in range(1, sections):
        more.append(
            pltpu.make_async_remote_copy(
                part.at[sec],
                part.at[sec],
                send2.at[off],
                recv2.at[off],
                device_id={"tm": lax.rem(sec + off, sections)},
                device_id_type=MESH,
            )
        )
    for copy in more:
        copy.start()
    for copy in copies:
        copy.wait_send()
    for copy in more:
        copy.wait_recv()
    total = part[0].astype(F32)
    for s in range(1, sections):
        total = total + part[s].astype(F32)
    high = total.astype(full.dtype)
    low = (total - high.astype(F32))[:, :128]
    lane = lax.broadcasted_iota(jnp.int32, (rows, PACK_COLS), 1)
    row = lax.broadcasted_iota(jnp.int32, (rows, PACK_COLS), 0) + me * rows
    low = jnp.concatenate([low, low, low], axis=1)
    spare = (row >= top) & (lane >= 256)
    full[me] = jnp.where(spare, low, high.astype(F32)).astype(full.dtype)
    last = []
    for off in range(1, group):
        last.append(
            pltpu.make_async_remote_copy(
                full.at[me],
                full.at[me],
                send3.at[off],
                recv3.at[off],
                device_id={"clip": lax.rem(me + off, group)},
                device_id_type=MESH,
            )
        )
    for copy in last:
        copy.start()
    for copy in more:
        copy.wait_send()
    for c in range(clips):
        store_out(c).wait()
    for d in range(2):

        @pl.when(place(d) < sections - 1)
        def _():
            for c in range(clips):
                hop(d, c).wait_send()

    for copy in last:
        copy.wait()
    summed = jnp.concatenate([full[g].astype(F32) for g in range(group)], axis=0)
    g_merge = summed[:top]
    g_head = summed[top : top + SUBPIX, :CHANNELS]

    def squares(v):
        return jnp.sum(jnp.sum(v * v, axis=0, keepdims=True), axis=1, keepdims=True)

    factor = jnp.minimum(1.0, CLIP_LIMIT / jnp.sqrt(squares(g_merge) + squares(g_head) + 1e-06))
    for i in range(3):
        gm_ref[:, i * PACK_COLS : (i + 1) * PACK_COLS] = (
            g_merge[i * CHANNELS : (i + 1) * CHANNELS] * factor
        )
    gh_ref[...] = g_head * factor
    end = top + SUBPIX
    loss_ref[...] = summed[end : end + 1, 0:1] + summed[end : end + 1, 256:257]


def on_device(features, flow_forward, flow_backward, *rest):
    weights, target = list(rest[:-1]), rest[-1]
    clips = features.shape[0]
    sections = lax.axis_size("tm")
    group = lax.axis_size("clip")
    scale = 1.0 / (clips * group * sections)
    held = [features, *(w[None] if w.ndim == 1 else w for w in weights), target]
    anywhere = pl.BlockSpec(memory_space=pl.ANY)
    vmem = pl.BlockSpec(memory_space=pltpu.VMEM)
    smem = pl.BlockSpec(memory_space=pltpu.SMEM)
    dma = pltpu.SemaphoreType.DMA
    rows = PACK_ROWS // group
    third = 3 * CHANNELS
    restored, grad_merge, grad_head, loss = pl.pallas_call(
        functools.partial(fused_kernel, group, sections, scale),
        out_shape=(
            jax.ShapeDtypeStruct((clips, 1, SUBPIX, PIXELS), BF),
            jax.ShapeDtypeStruct((CHANNELS, 18 * CHANNELS), F32),
            jax.ShapeDtypeStruct((SUBPIX, CHANNELS), F32),
            jax.ShapeDtypeStruct((1, 1), F32),
        ),
        in_specs=[smem] * 2 + [anywhere] * len(held),
        out_specs=[anywhere] + [vmem] * 3,
        scratch_shapes=[pltpu.VMEM(a.shape, a.dtype) for a in held]
        + [
            dma((len(held),)),
            pltpu.VMEM((clips, SUBPIX, PIXELS), BF),
            dma((clips,)),
            pltpu.VMEM((2, third, third), BF),
            pltpu.VMEM((2, third, third), BF),
            pltpu.VMEM((2, third, third), BF),
            pltpu.VMEM((2, CHANNELS, 1), F32),
            pltpu.VMEM((2, CHANNELS, 1), F32),
            pltpu.VMEM((PIXELS // TILE, WINDOW, TILE), BF),
            pltpu.VMEM((CHANNELS, PIXELS), F32),
            pltpu.VMEM((2, clips, CHANNELS, PIXELS + 2 * MARGIN), BF),
            pltpu.VMEM((2, clips, CHANNELS, PIXELS), BF),
            dma((2 * clips,)),
            dma((2 * clips,)),
            pltpu.VMEM((third, 6 * CHANNELS), F32),
            pltpu.VMEM((SUBPIX, CHANNELS), F32),
            pltpu.VMEM((1, 1), F32),
            pltpu.VMEM((group, rows, PACK_COLS), PART_TYPE),
            pltpu.VMEM((group, rows, PACK_COLS), PART_TYPE),
            pltpu.VMEM((sections, rows, PACK_COLS), PART_TYPE),
            pltpu.VMEM((group, rows, PACK_COLS), BF),
            dma((group,)),
            dma((group,)),
            dma((sections,)),
            dma((sections,)),
            dma((group,)),
            dma((group,)),
        ],
        compiler_params=pltpu.CompilerParams(
            collective_id=0, has_side_effects=True, vmem_limit_bytes=48 << 20
        ),
        name="step",
    )(flow_forward, flow_backward, *held)
    return (restored, grad_merge, grad_head, loss[0, 0])


def solution(mesh):
    split = P("clip", "tm", None, None)
    in_specs = (split,) * 3 + (P(),) * 12 + (split,)
    out_specs = (split, P(), P(), P())
    return jax.shard_map(
        on_device, mesh=mesh, in_specs=in_specs, out_specs=out_specs, check_vma=False
    )
```

```python
import functools

import jax
import jax.numpy as jnp
from jax import lax
from jax.experimental import pallas as pl
from jax.experimental.pallas import tpu as pltpu
from jax.sharding import PartitionSpec as P

CHANNELS = 64
SUBPIX = 48
WIDTH = 32
PIXELS = 1024
BLOCK = 8
REACH = 4
TILE = 256
MARGIN = REACH * WIDTH
WINDOW = TILE + 2 * MARGIN
CLIP_LIMIT = 128.0
LEAK = 0.1
PACK_ROWS = 256
PACK_COLS = 384
MESH = pl.DeviceIdType.MESH
BF = jnp.bfloat16
F32 = jnp.float32
PART_TYPE = F32


def roll_lanes(value, shift):
    return pltpu.roll(value, shift % PIXELS, 1)


def lane_masks():
    lane = lax.broadcasted_iota(jnp.int32, (1, PIXELS), 1)
    col = lane % WIDTH
    return (
        (col != 0),
        (col != WIDTH - 1),
        (lane >= WIDTH),
        (lane < PIXELS - WIDTH),
    )


def column_taps(value, masks):
    left = jnp.where(masks[0], roll_lanes(value, 1), 0.0)
    right = jnp.where(masks[1], roll_lanes(value, -1), 0.0)
    return [left.astype(BF), value.astype(BF), right.astype(BF)]


def row_sum(stacked, masks):
    up = jnp.where(masks[2], roll_lanes(stacked[:CHANNELS], WIDTH), 0.0)
    down = jnp.where(masks[3], roll_lanes(stacked[2 * CHANNELS :], -WIDTH), 0.0)
    return up + stacked[CHANNELS : 2 * CHANNELS] + down


def dot(a, b):
    return jnp.dot(a, b, preferred_element_type=F32)


def dot_t(a, b):
    return lax.dot_general(a, b, (((1,), (1,)), ((), ())), preferred_element_type=F32)


def stack_rows(weight):
    third = weight.shape[1] // 3
    return jnp.concatenate([weight[:, i * third : (i + 1) * third] for i in range(3)], axis=0)


def merge(hf, hb, target, w_merge, b_merge, w_head, b_head, scale, masks):
    taps_f = column_taps(hf.astype(F32), masks)
    taps_b = column_taps(hb.astype(F32), masks)
    joined = jnp.concatenate([t for pair in zip(taps_f, taps_b) for t in pair], axis=0)
    m = row_sum(dot(w_merge, joined), masks) + b_merge
    sig = jax.nn.sigmoid(m)
    active = (m * sig).astype(BF)
    out = dot(w_head, active) + b_head
    misfit = out - target.astype(F32)
    loss = jnp.sum(misfit * misfit, axis=0, keepdims=True)
    loss = jnp.sum(loss, axis=1, keepdims=True) * (0.5 * scale)
    err = (misfit * scale).astype(BF)
    g_head = dot_t(err, active)
    back = lax.dot_general(w_head, err, (((0,), (0,)), ((), ())), preferred_element_type=F32)
    d_m = (back * (sig * (1.0 + m * (1.0 - sig)))).astype(BF).astype(F32)
    above = jnp.where(masks[3], roll_lanes(d_m, -WIDTH), 0.0).astype(BF)
    below = jnp.where(masks[2], roll_lanes(d_m, WIDTH), 0.0).astype(BF)
    g_merge = dot_t(jnp.concatenate([above, d_m.astype(BF), below], axis=0), joined)
    return out.astype(BF), g_merge, g_head, loss


def window_cells(flow_ref, clip, start):
    lane = lax.broadcasted_iota(jnp.int32, (1, TILE), 1)
    row, col = lane // WIDTH, lane % WIDTH
    side = WIDTH // BLOCK
    first = start // TILE * side

    def offsets(part):
        value = jnp.full((1, TILE), flow_ref[clip, 0, part, first], jnp.int32)
        for b in range(1, side):
            value = jnp.where(col >= b * BLOCK, flow_ref[clip, 0, part, first + b], value)
        return value

    source_col = col + offsets(1)
    cell = (row + offsets(0) + REACH) * WIDTH + source_col
    return jnp.where((source_col >= 0) & (source_col < WIDTH), cell, -1)


def fused_kernel(group, sections, scale, *refs):
    n_in = 14
    flows = refs[:2]
    hbm_in = refs[2 : 2 + n_in]
    out_ref, gm_ref, gh_ref, loss_ref = refs[2 + n_in : 6 + n_in]
    held = refs[6 + n_in : 6 + 2 * n_in]
    (
        in_sem,
        out_buf,
        out_sem,
        w_g,
        w_x,
        w_out,
        b_in,
        b_out,
        one_hot,
        fixed,
        prior,
        state,
        hop_send,
        hop_recv,
        acc_gm,
        acc_gh,
        acc_loss,
        pack,
        got,
        part,
        full,
        send1,
        recv1,
        send2,
        recv2,
        send3,
        recv3,
    ) = refs[6 + 2 * n_in :]
    feat, wfi, bfi, wfo, bfo, wbi, bbi, wbo, bbo, wm, bm, wh, bh, target = held
    clips = feat.shape[0]
    rows = PACK_ROWS // group
    me = lax.axis_index("clip")
    sec = lax.axis_index("tm")

    loads = [
        pltpu.make_async_copy(a, b, in_sem.at[k]) for k, (a, b) in enumerate(zip(hbm_in, held))
    ]
    for load in loads:
        load.start()
    prior[...] = jnp.zeros_like(prior)
    barrier = pltpu.get_barrier_semaphore()
    for off in range(1, group):
        pl.semaphore_signal(
            barrier, 1, device_id={"clip": lax.rem(me + off, group)}, device_id_type=MESH
        )
    for off in range(1, sections):
        pl.semaphore_signal(
            barrier, 1, device_id={"tm": lax.rem(sec + off, sections)}, device_id_type=MESH
        )
    for load in loads:
        load.wait()

    masks = lane_masks()
    eye = lax.broadcasted_iota(jnp.int32, (CHANNELS, CHANNELS), 0) == lax.broadcasted_iota(
        jnp.int32, (CHANNELS, CHANNELS), 1
    )

    def column(row):
        n = row.shape[1]
        return jnp.sum(jnp.where(eye[:n, :n], row, 0.0), axis=1, keepdims=True)

    def part_rows(weight, first):
        return jnp.concatenate(
            [
                jnp.concatenate(
                    [
                        weight[:, (3 * dy + dx) * 128 + first : (3 * dy + dx) * 128 + first + 64]
                        for dx in range(3)
                    ],
                    axis=1,
                )
                for dy in range(3)
            ],
            axis=0,
        )

    for d, (wi, bi, wo, bo) in enumerate(((wfi, bfi, wfo, bfo), (wbi, bbi, wbo, bbo))):
        w_g[d] = part_rows(wi[...], 0)
        w_x[d] = part_rows(wi[...], CHANNELS)
        w_out[d] = stack_rows(wo[...])
        b_in[d] = column(bi[...])
        b_out[d] = column(bo[...])
    pl.semaphore_wait(barrier, group + sections - 2)

    window_cell = lax.broadcasted_iota(jnp.int32, (WINDOW, TILE), 0)
    inner = pl.ds(MARGIN, PIXELS)

    def hop(d, c):
        slot = d * clips + c
        return pltpu.make_async_remote_copy(
            state.at[d, c],
            prior.at[d, c, :, inner],
            hop_send.at[slot],
            hop_recv.at[slot],
            device_id={"tm": sec + 1 - 2 * d},
            device_id_type=MESH,
        )

    def place(d):
        return jnp.where(d == 0, sec, sections - 1 - sec)

    def step(d, c):
        for k, start in enumerate(range(0, PIXELS, TILE)):
            cells = jnp.where(
                d == 0, window_cells(flows[0], c, start), window_cells(flows[1], c, start)
            )
            one_hot[k] = (window_cell == cells).astype(F32).astype(BF)
        taps_x = jnp.concatenate(column_taps(feat[c, 0].astype(F32), masks), axis=0)
        fixed[...] = row_sum(dot(w_x[d], taps_x), masks) + b_in[d]

        @pl.when(place(d) > 0)
        def _():
            hop(d, c).wait_recv()

        warped = jnp.concatenate(
            [
                dot(prior[d, c, :, start : start + WINDOW], one_hot[start // TILE])
                for start in range(0, PIXELS, TILE)
            ],
            axis=1,
        )
        taps_g = jnp.concatenate(column_taps(warped, masks), axis=0)
        hidden = row_sum(dot(w_g[d], taps_g), masks) + fixed[...]
        hidden = jnp.where(hidden >= 0, hidden, LEAK * hidden).astype(BF).astype(F32)
        taps_a = jnp.concatenate(column_taps(hidden, masks), axis=0)
        update = row_sum(dot(w_out[d], taps_a), masks) + b_out[d]
        state[d, c] = (warped + update).astype(BF)

        @pl.when(place(d) < sections - 1)
        def _():
            hop(d, c).start()

    early = jnp.where(2 * sec < sections, 0, 1)

    def first_turn(c, carry):
        step(early, c)
        return carry

    lax.fori_loop(0, clips, first_turn, 0)
    acc_gm[...] = jnp.zeros_like(acc_gm)
    acc_gh[...] = jnp.zeros_like(acc_gh)
    acc_loss[...] = jnp.zeros_like(acc_loss)
    w_merge = stack_rows(wm[...])
    b_merge = column(bm[...])
    b_head = column(bh[...])

    def store_out(c):
        return pltpu.make_async_copy(out_buf.at[c], out_ref.at[c, 0], out_sem.at[c])

    def last_turn(c, carry):
        step(1 - early, c)
        out, g_merge, g_head, loss = merge(
            state[0, c],
            state[1, c],
            target[c, 0],
            w_merge,
            b_merge,
            wh[...],
            b_head,
            scale,
            masks,
        )
        out_buf[c] = out
        store_out(c).start()
        acc_gm[...] += g_merge
        acc_gh[...] += g_head
        acc_loss[...] += loss
        return carry

    lax.fori_loop(0, clips, last_turn, 0)

    top = 3 * CHANNELS
    g_merge = acc_gm[...]
    extra = jnp.concatenate(
        [
            jnp.concatenate(
                [acc_gh[...], jnp.zeros((SUBPIX, CHANNELS), F32)],
                axis=1,
            ),
            jnp.broadcast_to(acc_loss[...], (PACK_ROWS - top - SUBPIX, 128)),
        ],
        axis=0,
    )
    extra = jnp.concatenate(
        [extra, jnp.zeros((PACK_ROWS - top, PACK_COLS - 128), F32)], axis=1
    )
    packed = jnp.concatenate([g_merge, extra], axis=0)
    for g in range(group):
        pack[g] = packed[g * rows : (g + 1) * rows].astype(pack.dtype)

    copies = []
    for off in range(1, group):
        peer = lax.rem(me + off, group)
        copies.append(
            pltpu.make_async_remote_copy(
                pack.at[peer],
                got.at[off],
                send1.at[off],
                recv1.at[off],
                device_id={"clip": peer},
                device_id_type=MESH,
            )
        )
    for copy in copies:
        copy.start()
    total = pack[me].astype(F32)
    for off, copy in enumerate(copies, 1):
        copy.wait_recv()
        total = total + got[off].astype(F32)
    part[sec] = total.astype(part.dtype)
    more = []
    for off in range(1, sections):
        more.append(
            pltpu.make_async_remote_copy(
                part.at[sec],
                part.at[sec],
                send2.at[off],
                recv2.at[off],
                device_id={"tm": lax.rem(sec + off, sections)},
                device_id_type=MESH,
            )
        )
    for copy in more:
        copy.start()
    for copy in copies:
        copy.wait_send()
    for copy in more:
        copy.wait_recv()
    total = part[0].astype(F32)
    for s in range(1, sections):
        total = total + part[s].astype(F32)
    high = total.astype(full.dtype)
    low = (total - high.astype(F32))[:, :128]
    lane = lax.broadcasted_iota(jnp.int32, (rows, PACK_COLS), 1)
    row = lax.broadcasted_iota(jnp.int32, (rows, PACK_COLS), 0) + me * rows
    low = jnp.concatenate([low, low, low], axis=1)
    spare = (row >= top) & (lane >= 256)
    full[me] = jnp.where(spare, low, high.astype(F32)).astype(full.dtype)
    last = []
    for off in range(1, group):
        last.append(
            pltpu.make_async_remote_copy(
                full.at[me],
                full.at[me],
                send3.at[off],
                recv3.at[off],
                device_id={"clip": lax.rem(me + off, group)},
                device_id_type=MESH,
            )
        )
    for copy in last:
        copy.start()
    for copy in more:
        copy.wait_send()
    for c in range(clips):
        store_out(c).wait()
    for d in range(2):

        @pl.when(place(d) < sections - 1)
        def _():
            for c in range(clips):
                hop(d, c).wait_send()

    for copy in last:
        copy.wait()
    summed = jnp.concatenate([full[g].astype(F32) for g in range(group)], axis=0)
    g_merge = summed[:top]
    g_head = summed[top : top + SUBPIX, :CHANNELS]

    def squares(v):
        return jnp.sum(jnp.sum(v * v, axis=0, keepdims=True), axis=1, keepdims=True)

    factor = jnp.minimum(1.0, CLIP_LIMIT / jnp.sqrt(squares(g_merge) + squares(g_head) + 1e-06))
    for i in range(3):
        gm_ref[:, i * PACK_COLS : (i + 1) * PACK_COLS] = (
            g_merge[i * CHANNELS : (i + 1) * CHANNELS] * factor
        )
    gh_ref[...] = g_head * factor
    end = top + SUBPIX
    loss_ref[...] = summed[end : end + 1, 0:1] + summed[end : end + 1, 256:257]


def on_device(features, flow_forward, flow_backward, *rest):
    weights, target = list(rest[:-1]), rest[-1]
    clips = features.shape[0]
    sections = lax.axis_size("tm")
    group = lax.axis_size("clip")
    scale = 1.0 / (clips * group * sections)
    held = [features, *(w[None] if w.ndim == 1 else w for w in weights), target]
    anywhere = pl.BlockSpec(memory_space=pltpu.HBM)
    vmem = pl.BlockSpec(memory_space=pltpu.VMEM)
    smem = pl.BlockSpec(memory_space=pltpu.SMEM)
    dma = pltpu.SemaphoreType.DMA
    rows = PACK_ROWS // group
    third = 3 * CHANNELS
    restored, grad_merge, grad_head, loss = pl.pallas_call(
        functools.partial(fused_kernel, group, sections, scale),
        out_shape=(
            jax.ShapeDtypeStruct((clips, 1, SUBPIX, PIXELS), BF),
            jax.ShapeDtypeStruct((CHANNELS, 18 * CHANNELS), F32),
            jax.ShapeDtypeStruct((SUBPIX, CHANNELS), F32),
            jax.ShapeDtypeStruct((1, 1), F32),
        ),
        in_specs=[smem] * 2 + [anywhere] * len(held),
        out_specs=[anywhere] + [vmem] * 3,
        scratch_shapes=[pltpu.VMEM(a.shape, a.dtype) for a in held]
        + [
            dma((len(held),)),
            pltpu.VMEM((clips, SUBPIX, PIXELS), BF),
            dma((clips,)),
            pltpu.VMEM((2, third, third), BF),
            pltpu.VMEM((2, third, third), BF),
            pltpu.VMEM((2, third, third), BF),
            pltpu.VMEM((2, CHANNELS, 1), F32),
            pltpu.VMEM((2, CHANNELS, 1), F32),
            pltpu.VMEM((PIXELS // TILE, WINDOW, TILE), BF),
            pltpu.VMEM((CHANNELS, PIXELS), F32),
            pltpu.VMEM((2, clips, CHANNELS, PIXELS + 2 * MARGIN), BF),
            pltpu.VMEM((2, clips, CHANNELS, PIXELS), BF),
            dma((2 * clips,)),
            dma((2 * clips,)),
            pltpu.VMEM((third, 6 * CHANNELS), F32),
            pltpu.VMEM((SUBPIX, CHANNELS), F32),
            pltpu.VMEM((1, 1), F32),
            pltpu.VMEM((group, rows, PACK_COLS), PART_TYPE),
            pltpu.VMEM((group, rows, PACK_COLS), PART_TYPE),
            pltpu.VMEM((sections, rows, PACK_COLS), PART_TYPE),
            pltpu.VMEM((group, rows, PACK_COLS), BF),
            dma((group,)),
            dma((group,)),
            dma((sections,)),
            dma((sections,)),
            dma((group,)),
            dma((group,)),
        ],
        compiler_params=pltpu.CompilerParams(
            collective_id=0, has_side_effects=True, vmem_limit_bytes=63 << 20
        ),
        name="step",
    )(flow_forward, flow_backward, *held)
    return (restored, grad_merge, grad_head, loss[0, 0])


def solution(mesh):
    split = P("clip", "tm", None, None)
    in_specs = (split,) * 3 + (P(),) * 12 + (split,)
    out_specs = (split, P(), P(), P())
    return jax.shard_map(
        on_device, mesh=mesh, in_specs=in_specs, out_specs=out_specs, check_vma=False
    )
```

```python
import functools

import jax
import jax.numpy as jnp
from jax import lax
from jax.experimental import pallas as pl
from jax.experimental.pallas import tpu as pltpu
from jax.sharding import PartitionSpec as P

CHANNELS = 64
SUBPIX = 48
WIDTH = 32
PIXELS = 1024
BLOCK = 8
REACH = 4
TILE = 256
MARGIN = REACH * WIDTH
WINDOW = TILE + 2 * MARGIN
CLIP_LIMIT = 128.0
LEAK = 0.1
PACK_ROWS = 256
PACK_COLS = 384
MESH = pl.DeviceIdType.MESH
BF = jnp.bfloat16
F32 = jnp.float32
PART_TYPE = BF


def roll_lanes(value, shift):
    return pltpu.roll(value, shift % PIXELS, 1)


def lane_masks():
    lane = lax.broadcasted_iota(jnp.int32, (1, PIXELS), 1)
    col = lane % WIDTH
    return (
        (col != 0),
        (col != WIDTH - 1),
        (lane >= WIDTH),
        (lane < PIXELS - WIDTH),
    )


def column_taps(value, masks):
    left = jnp.where(masks[0], roll_lanes(value, 1), 0.0)
    right = jnp.where(masks[1], roll_lanes(value, -1), 0.0)
    return [left.astype(BF), value.astype(BF), right.astype(BF)]


def row_sum(stacked, masks):
    up = jnp.where(masks[2], roll_lanes(stacked[:CHANNELS], WIDTH), 0.0)
    down = jnp.where(masks[3], roll_lanes(stacked[2 * CHANNELS :], -WIDTH), 0.0)
    return up + stacked[CHANNELS : 2 * CHANNELS] + down


def dot(a, b):
    return jnp.dot(a, b, preferred_element_type=F32)


def dot_t(a, b):
    return lax.dot_general(a, b, (((1,), (1,)), ((), ())), preferred_element_type=F32)


def stack_rows(weight):
    third = weight.shape[1] // 3
    return jnp.concatenate([weight[:, i * third : (i + 1) * third] for i in range(3)], axis=0)


def merge(hf, hb, target, w_merge, b_merge, w_head, b_head, scale, masks):
    taps_f = column_taps(hf.astype(F32), masks)
    taps_b = column_taps(hb.astype(F32), masks)
    joined = jnp.concatenate([t for pair in zip(taps_f, taps_b) for t in pair], axis=0)
    m = row_sum(dot(w_merge, joined), masks) + b_merge
    sig = jax.nn.sigmoid(m)
    active = (m * sig).astype(BF)
    out = dot(w_head, active) + b_head
    misfit = out - target.astype(F32)
    loss = jnp.sum(misfit * misfit, axis=0, keepdims=True)
    loss = jnp.sum(loss, axis=1, keepdims=True) * (0.5 * scale)
    err = (misfit * scale).astype(BF)
    g_head = dot_t(err, active)
    back = lax.dot_general(w_head, err, (((0,), (0,)), ((), ())), preferred_element_type=F32)
    d_m = (back * (sig * (1.0 + m * (1.0 - sig)))).astype(BF).astype(F32)
    above = jnp.where(masks[3], roll_lanes(d_m, -WIDTH), 0.0).astype(BF)
    below = jnp.where(masks[2], roll_lanes(d_m, WIDTH), 0.0).astype(BF)
    g_merge = dot_t(jnp.concatenate([above, d_m.astype(BF), below], axis=0), joined)
    return out.astype(BF), g_merge, g_head, loss


def window_cells(flow_ref, clip, start):
    lane = lax.broadcasted_iota(jnp.int32, (1, TILE), 1)
    row, col = lane // WIDTH, lane % WIDTH
    side = WIDTH // BLOCK
    first = start // TILE * side

    def offsets(part):
        value = jnp.full((1, TILE), flow_ref[clip, 0, part, first], jnp.int32)
        for b in range(1, side):
            value = jnp.where(col >= b * BLOCK, flow_ref[clip, 0, part, first + b], value)
        return value

    source_col = col + offsets(1)
    cell = (row + offsets(0) + REACH) * WIDTH + source_col
    return jnp.where((source_col >= 0) & (source_col < WIDTH), cell, -1)


def fused_kernel(group, sections, scale, *refs):
    n_in = 14
    flows = refs[:2]
    hbm_in = refs[2 : 2 + n_in]
    out_ref, gm_ref, gh_ref, loss_ref = refs[2 + n_in : 6 + n_in]
    held = refs[6 + n_in : 6 + 2 * n_in]
    (
        in_sem,
        out_buf,
        out_sem,
        w_g,
        w_x,
        w_out,
        b_in,
        b_out,
        one_hot,
        fixed,
        prior,
        state,
        hop_send,
        hop_recv,
        acc_gm,
        acc_gh,
        acc_loss,
        pack,
        got,
        part,
        full,
        send1,
        recv1,
        send2,
        recv2,
        send3,
        recv3,
    ) = refs[6 + 2 * n_in :]
    feat, wfi, bfi, wfo, bfo, wbi, bbi, wbo, bbo, wm, bm, wh, bh, target = held
    clips = feat.shape[0]
    rows = PACK_ROWS // group
    me = lax.axis_index("clip")
    sec = lax.axis_index("tm")

    loads = [
        pltpu.make_async_copy(a, b, in_sem.at[k]) for k, (a, b) in enumerate(zip(hbm_in, held))
    ]
    for load in loads:
        load.start()
    prior[...] = jnp.zeros_like(prior)
    barrier = pltpu.get_barrier_semaphore()
    for off in range(1, group):
        pl.semaphore_signal(
            barrier, 1, device_id={"clip": lax.rem(me + off, group)}, device_id_type=MESH
        )
    for off in range(1, sections):
        pl.semaphore_signal(
            barrier, 1, device_id={"tm": lax.rem(sec + off, sections)}, device_id_type=MESH
        )
    for load in loads:
        load.wait()

    masks = lane_masks()
    eye = lax.broadcasted_iota(jnp.int32, (CHANNELS, CHANNELS), 0) == lax.broadcasted_iota(
        jnp.int32, (CHANNELS, CHANNELS), 1
    )

    def column(row):
        n = row.shape[1]
        return jnp.sum(jnp.where(eye[:n, :n], row, 0.0), axis=1, keepdims=True)

    def part_rows(weight, first):
        return jnp.concatenate(
            [
                jnp.concatenate(
                    [
                        weight[:, (3 * dy + dx) * 128 + first : (3 * dy + dx) * 128 + first + 64]
                        for dx in range(3)
                    ],
                    axis=1,
                )
                for dy in range(3)
            ],
            axis=0,
        )

    for d, (wi, bi, wo, bo) in enumerate(((wfi, bfi, wfo, bfo), (wbi, bbi, wbo, bbo))):
        w_g[d] = part_rows(wi[...], 0)
        w_x[d] = part_rows(wi[...], CHANNELS)
        w_out[d] = stack_rows(wo[...])
        b_in[d] = column(bi[...])
        b_out[d] = column(bo[...])
    pl.semaphore_wait(barrier, group + sections - 2)

    window_cell = lax.broadcasted_iota(jnp.int32, (WINDOW, TILE), 0)
    inner = pl.ds(MARGIN, PIXELS)

    def hop(d, c):
        slot = d * clips + c
        return pltpu.make_async_remote_copy(
            state.at[d, c],
            prior.at[d, c, :, inner],
            hop_send.at[slot],
            hop_recv.at[slot],
            device_id={"tm": sec + 1 - 2 * d},
            device_id_type=MESH,
        )

    def place(d):
        return jnp.where(d == 0, sec, sections - 1 - sec)

    def step(d, c):
        for k, start in enumerate(range(0, PIXELS, TILE)):
            cells = jnp.where(
                d == 0, window_cells(flows[0], c, start), window_cells(flows[1], c, start)
            )
            one_hot[k] = (window_cell == cells).astype(F32).astype(BF)
        taps_x = jnp.concatenate(column_taps(feat[c, 0].astype(F32), masks), axis=0)
        fixed[...] = row_sum(dot(w_x[d], taps_x), masks) + b_in[d]

        @pl.when(place(d) > 0)
        def _():
            hop(d, c).wait_recv()

        warped = jnp.concatenate(
            [
                dot(prior[d, c, :, start : start + WINDOW], one_hot[start // TILE])
                for start in range(0, PIXELS, TILE)
            ],
            axis=1,
        )
        taps_g = jnp.concatenate(column_taps(warped, masks), axis=0)
        hidden = row_sum(dot(w_g[d], taps_g), masks) + fixed[...]
        hidden = jnp.where(hidden >= 0, hidden, LEAK * hidden).astype(BF).astype(F32)
        taps_a = jnp.concatenate(column_taps(hidden, masks), axis=0)
        update = row_sum(dot(w_out[d], taps_a), masks) + b_out[d]
        state[d, c] = (warped + update).astype(BF)

        @pl.when(place(d) < sections - 1)
        def _():
            hop(d, c).start()

    early = jnp.where(2 * sec < sections, 0, 1)

    def first_turn(c, carry):
        step(early, c)
        return carry

    lax.fori_loop(0, clips, first_turn, 0)
    acc_gm[...] = jnp.zeros_like(acc_gm)
    acc_gh[...] = jnp.zeros_like(acc_gh)
    acc_loss[...] = jnp.zeros_like(acc_loss)
    w_merge = stack_rows(wm[...])
    b_merge = column(bm[...])
    b_head = column(bh[...])

    def store_out(c):
        return pltpu.make_async_copy(out_buf.at[c], out_ref.at[c, 0], out_sem.at[c])

    def last_turn(c, carry):
        step(1 - early, c)
        out, g_merge, g_head, loss = merge(
            state[0, c],
            state[1, c],
            target[c, 0],
            w_merge,
            b_merge,
            wh[...],
            b_head,
            scale,
            masks,
        )
        out_buf[c] = out
        store_out(c).start()
        acc_gm[...] += g_merge
        acc_gh[...] += g_head
        acc_loss[...] += loss
        return carry

    lax.fori_loop(0, clips, last_turn, 0)

    top = 3 * CHANNELS
    g_merge = acc_gm[...]
    extra = jnp.concatenate(
        [
            jnp.concatenate(
                [acc_gh[...], jnp.zeros((SUBPIX, CHANNELS), F32)],
                axis=1,
            ),
            jnp.broadcast_to(acc_loss[...], (PACK_ROWS - top - SUBPIX, 128)),
        ],
        axis=0,
    )
    extra = jnp.concatenate(
        [extra, jnp.zeros((PACK_ROWS - top, PACK_COLS - 128), F32)], axis=1
    )
    packed = jnp.concatenate([g_merge, extra], axis=0)
    for g in range(group):
        pack[g] = packed[g * rows : (g + 1) * rows].astype(pack.dtype)

    copies = []
    for off in range(1, group):
        peer = lax.rem(me + off, group)
        copies.append(
            pltpu.make_async_remote_copy(
                pack.at[peer],
                got.at[off],
                send1.at[off],
                recv1.at[off],
                device_id={"clip": peer},
                device_id_type=MESH,
            )
        )
    for copy in copies:
        copy.start()
    total = pack[me].astype(F32)
    for off, copy in enumerate(copies, 1):
        copy.wait_recv()
        total = total + got[off].astype(F32)
    part[sec] = total.astype(part.dtype)
    more = []
    for off in range(1, sections):
        more.append(
            pltpu.make_async_remote_copy(
                part.at[sec],
                part.at[sec],
                send2.at[off],
                recv2.at[off],
                device_id={"tm": lax.rem(sec + off, sections)},
                device_id_type=MESH,
            )
        )
    for copy in more:
        copy.start()
    for copy in copies:
        copy.wait_send()
    for copy in more:
        copy.wait_recv()
    total = part[0].astype(F32)
    for s in range(1, sections):
        total = total + part[s].astype(F32)
    high = total.astype(full.dtype)
    low = (total - high.astype(F32))[:, :128]
    lane = lax.broadcasted_iota(jnp.int32, (rows, PACK_COLS), 1)
    row = lax.broadcasted_iota(jnp.int32, (rows, PACK_COLS), 0) + me * rows
    low = jnp.concatenate([low, low, low], axis=1)
    spare = (row >= top) & (lane >= 256)
    full[me] = jnp.where(spare, low, high.astype(F32)).astype(full.dtype)
    last = []
    for off in range(1, group):
        last.append(
            pltpu.make_async_remote_copy(
                full.at[me],
                full.at[me],
                send3.at[off],
                recv3.at[off],
                device_id={"clip": lax.rem(me + off, group)},
                device_id_type=MESH,
            )
        )
    for copy in last:
        copy.start()
    for copy in more:
        copy.wait_send()
    for c in range(clips):
        store_out(c).wait()
    for d in range(2):

        @pl.when(place(d) < sections - 1)
        def _():
            for c in range(clips):
                hop(d, c).wait_send()

    for copy in last:
        copy.wait()
    summed = jnp.concatenate([full[g].astype(F32) for g in range(group)], axis=0)
    g_merge = summed[:top]
    g_head = summed[top : top + SUBPIX, :CHANNELS]

    def squares(v):
        return jnp.sum(jnp.sum(v * v, axis=0, keepdims=True), axis=1, keepdims=True)

    factor = jnp.minimum(1.0, CLIP_LIMIT / jnp.sqrt(squares(g_merge) + squares(g_head) + 1e-06))
    for i in range(3):
        gm_ref[:, i * PACK_COLS : (i + 1) * PACK_COLS] = (
            g_merge[i * CHANNELS : (i + 1) * CHANNELS] * factor
        )
    gh_ref[...] = g_head * factor
    end = top + SUBPIX
    loss_ref[...] = summed[end : end + 1, 0:1] + summed[end : end + 1, 256:257]


def finish_kernel(*refs):
    n = (len(refs) - 2) // 3
    in_sem, out_sem = refs[-2:]
    held = refs[2 * n : 3 * n]
    loads = [pltpu.make_async_copy(refs[k], held[k], in_sem.at[k]) for k in range(n)]
    stores = [pltpu.make_async_copy(held[k], refs[n + k], out_sem.at[k]) for k in range(n)]
    for load in loads:
        load.start()
    for load, store in zip(loads, stores):
        load.wait()
        store.start()
    for store in stores:
        store.wait()


def on_device(features, flow_forward, flow_backward, *rest):
    weights, target = list(rest[:-1]), rest[-1]
    clips = features.shape[0]
    sections = lax.axis_size("tm")
    group = lax.axis_size("clip")
    scale = 1.0 / (clips * group * sections)
    held = [features, *(w[None] if w.ndim == 1 else w for w in weights), target]
    anywhere = pl.BlockSpec(memory_space=pltpu.HBM)
    vmem = pl.BlockSpec(memory_space=pltpu.VMEM)
    smem = pl.BlockSpec(memory_space=pltpu.SMEM)
    dma = pltpu.SemaphoreType.DMA
    rows = PACK_ROWS // group
    third = 3 * CHANNELS
    restored, grad_merge, grad_head, loss = pl.pallas_call(
        functools.partial(fused_kernel, group, sections, scale),
        out_shape=(
            jax.ShapeDtypeStruct((clips, 1, SUBPIX, PIXELS), BF),
            jax.ShapeDtypeStruct((CHANNELS, 18 * CHANNELS), F32),
            jax.ShapeDtypeStruct((SUBPIX, CHANNELS), F32),
            jax.ShapeDtypeStruct((1, 1), F32),
        ),
        in_specs=[smem] * 2 + [anywhere] * len(held),
        out_specs=[anywhere] + [vmem] * 3,
        scratch_shapes=[pltpu.VMEM(a.shape, a.dtype) for a in held]
        + [
            dma((len(held),)),
            pltpu.VMEM((clips, SUBPIX, PIXELS), BF),
            dma((clips,)),
            pltpu.VMEM((2, third, third), BF),
            pltpu.VMEM((2, third, third), BF),
            pltpu.VMEM((2, third, third), BF),
            pltpu.VMEM((2, CHANNELS, 1), F32),
            pltpu.VMEM((2, CHANNELS, 1), F32),
            pltpu.VMEM((PIXELS // TILE, WINDOW, TILE), BF),
            pltpu.VMEM((CHANNELS, PIXELS), F32),
            pltpu.VMEM((2, clips, CHANNELS, PIXELS + 2 * MARGIN), BF),
            pltpu.VMEM((2, clips, CHANNELS, PIXELS), BF),
            dma((2 * clips,)),
            dma((2 * clips,)),
            pltpu.VMEM((third, 6 * CHANNELS), F32),
            pltpu.VMEM((SUBPIX, CHANNELS), F32),
            pltpu.VMEM((1, 1), F32),
            pltpu.VMEM((group, rows, PACK_COLS), PART_TYPE),
            pltpu.VMEM((group, rows, PACK_COLS), PART_TYPE),
            pltpu.VMEM((sections, rows, PACK_COLS), PART_TYPE),
            pltpu.VMEM((group, rows, PACK_COLS), BF),
            dma((group,)),
            dma((group,)),
            dma((sections,)),
            dma((sections,)),
            dma((group,)),
            dma((group,)),
        ],
        compiler_params=pltpu.CompilerParams(
            collective_id=0, has_side_effects=True, vmem_limit_bytes=63 << 20
        ),
        name="step",
    )(flow_forward, flow_backward, *held)
    made = (restored, grad_merge, grad_head, loss)
    restored, grad_merge, grad_head, loss = pl.pallas_call(
        finish_kernel,
        out_shape=tuple(jax.ShapeDtypeStruct(a.shape, a.dtype) for a in made),
        in_specs=[anywhere] * 4,
        out_specs=[anywhere] * 4,
        scratch_shapes=[pltpu.VMEM(a.shape, a.dtype) for a in made] + [dma((4,)), dma((4,))],
        compiler_params=pltpu.CompilerParams(vmem_limit_bytes=63 << 20),
        name="finish",
    )(*made)
    return (restored, grad_merge, grad_head, loss[0, 0])


def solution(mesh):
    split = P("clip", "tm", None, None)
    in_specs = (split,) * 3 + (P(),) * 12 + (split,)
    out_specs = (split, P(), P(), P())
    return jax.shard_map(
        on_device, mesh=mesh, in_specs=in_specs, out_specs=out_specs, check_vma=False
    )
```
